32 devices in a mesh: groups: 2 (over y), seq: 8 (over z, x), heads: 2 (over core).
Axes of the slice: x: 2, y: 2, z: 4, core: 2. Of those that a mesh axis runs over, the one named last changes fastest.
Arguments:
- queries: bfloat16 [8192, 16, 128], P(('groups', 'seq'), 'heads'), parts along dimension 0, may hold values from -128 to 128
- keys: bfloat16 [8192, 16, 128], P(('groups', 'seq'), 'heads'), parts along dimension 0, may hold values from -128 to 128
- values: bfloat16 [8192, 16, 128], P(('groups', 'seq'), 'heads'), parts along dimension 0, may hold values from -6 to 6
Outputs:
- attended: bfloat16 [8192, 16, 128], P(('groups', 'seq'), 'heads'), parts along dimension 0
The draws below stay inside these ranges and needn't reach their ends.
There are 2 independent parts, one for each index of `groups`. The reference program is written for one: setup_inputs(seed, part) draws one part's arguments, and reference() takes and returns one part's arrays. A program takes and returns all parts, laid end to end along the dimension named above; each array names one. Nothing has to cross between parts.
All inputs are finite; a program needn't handle non-finite values.
Results may differ from the reference program's by a relative error of at most 0.0055.
Values may be sent and summed in bfloat16 or wider, within the bound.
A program may use at most 128 MiB of HBM per device.

```python
import math
import jax
import jax.numpy as jnp
from jax import lax

HEADS = 16
HD = 128
BLOCK = 64
LENGTH = 4096


def paired_fields(key):
    shape = (LENGTH, HEADS, HD)
    queries = jnp.clip(jax.random.normal(jax.random.fold_in(key, 101), shape, jnp.float32), -5.0, 5.0)
    keys = jnp.clip(jax.random.normal(jax.random.fold_in(key, 102), shape, jnp.float32), -5.0, 5.0)
    return (queries, keys)


def draw_queries(key, part):
    return paired_fields(key)[0].astype(jnp.bfloat16)


def draw_keys(key, part):
    return paired_fields(key)[1].astype(jnp.bfloat16)


def block_scale(own_key, extent, shards, smallest, largest):
    factor_of, own = 1.0, jax.random.fold_in(own_key, 6)
    for axis_at, parts in shards:
        draws = jnp.exp(jax.random.uniform(jax.random.fold_in(own, axis_at), (parts,), jnp.float32, smallest / len(shards), largest / len(shards)))
        factor_of = factor_of * jnp.repeat(draws, extent[axis_at] // parts).reshape([-1 if axis == axis_at else 1 for axis in range(len(extent))])
    return factor_of


def bell_draw(stream_key, extent, scale, bound, pieces=(), kind=jnp.bfloat16):
    result = scale * jax.random.normal(stream_key, extent, jnp.float32)
    if pieces:
        result = result * block_scale(stream_key, extent, pieces, -0.22, 0.18)
    return jnp.clip(result, -bound, bound).astype(kind)


def setup_inputs(seed: int = 0, part: int = 0) -> dict:
    key_of = jax.random.split(jax.random.key(seed), 4)
    part_splits = jax.random.split(jax.random.fold_in(key_of[3], part), 4)
    return {
        "queries": draw_queries(jax.random.fold_in(jax.random.fold_in(key_of[3], part), 71), part),
        "keys": draw_keys(jax.random.fold_in(jax.random.fold_in(key_of[3], part), 71), part),
        "values": bell_draw(part_splits[2], (LENGTH, HEADS, HD), 1.0, 6.0, ((0, 8), (1, 2))),
    }


neg_big = -1e+30
log_two = math.log(2.0)

def pool_rows(block, factor):
    count = block.shape[0] // factor
    grouped = block.astype(jnp.float32).reshape(count, factor, block.shape[1], block.shape[2])
    return lax.optimization_barrier(jnp.mean(grouped, axis=1)).astype(jnp.bfloat16)

def level_scores(query_block, key_rows, valid, bias):
    scores = jnp.einsum('qhd,khd->hqk', query_block.astype(jnp.float32), key_rows.astype(jnp.float32))
    scores = scores / math.sqrt(query_block.shape[2]) + bias
    return jnp.where(valid[None], scores, neg_big)

def reference(queries, keys, values):
    length, heads, width = queries.shape
    quad = 4 * BLOCK
    padding = jnp.zeros((BLOCK, heads, width), jnp.bfloat16)
    pooled_k = [pool_rows(keys, 2 ** level) for level in (1, 2, 3)]
    pooled_v = [pool_rows(values, 2 ** level) for level in (1, 2, 3)]
    ext0_k = jnp.concatenate([padding, keys], 0)
    ext0_v = jnp.concatenate([padding, values], 0)
    ext1_k = jnp.concatenate([padding, pooled_k[0]], 0)
    ext1_v = jnp.concatenate([padding, pooled_v[0]], 0)
    ext2_k = jnp.concatenate([padding, pooled_k[1]], 0)
    ext2_v = jnp.concatenate([padding, pooled_v[1]], 0)
    coarse_rows = jnp.arange(length // 8, dtype=jnp.int32)

    def one_block(blk):
        start = (blk * quad).astype(jnp.int32)
        posit = start + jnp.arange(quad, dtype=jnp.int32)
        bound0 = (posit // BLOCK - 1) * BLOCK
        bound1 = (posit // (2 * BLOCK) - 1) * 2 * BLOCK
        bound2 = (posit // quad - 1) * quad
        query_block = lax.dynamic_slice_in_dim(queries, start, quad, 0)
        tokens0 = start - BLOCK + jnp.arange(quad + BLOCK, dtype=jnp.int32)
        rows1 = start // 2 - BLOCK + jnp.arange(quad // 2 + BLOCK, dtype=jnp.int32)
        rows2 = start // 4 - BLOCK + jnp.arange(quad // 4 + BLOCK, dtype=jnp.int32)
        key0 = lax.dynamic_slice_in_dim(ext0_k, start, quad + BLOCK, 0)
        val0 = lax.dynamic_slice_in_dim(ext0_v, start, quad + BLOCK, 0)
        key1 = lax.dynamic_slice_in_dim(ext1_k, (start // 2).astype(jnp.int32), quad // 2 + BLOCK, 0)
        val1 = lax.dynamic_slice_in_dim(ext1_v, (start // 2).astype(jnp.int32), quad // 2 + BLOCK, 0)
        key2 = lax.dynamic_slice_in_dim(ext2_k, (start // 4).astype(jnp.int32), quad // 4 + BLOCK, 0)
        val2 = lax.dynamic_slice_in_dim(ext2_v, (start // 4).astype(jnp.int32), quad // 4 + BLOCK, 0)
        valid0 = (tokens0 >= 0)[None] & (tokens0[None] >= bound0[:, None]) & (tokens0[None] <= posit[:, None])
        valid1 = (rows1 >= 0)[None] & (2 * rows1[None] >= bound1[:, None]) & (2 * rows1[None] + 2 <= bound0[:, None])
        valid2 = (rows2 >= 0)[None] & (4 * rows2[None] >= bound2[:, None]) & (4 * rows2[None] + 4 <= bound1[:, None])
        valid3 = 8 * coarse_rows[None] + 8 <= bound2[:, None]
        scores = jnp.concatenate([level_scores(query_block, key0, valid0, 0.0), level_scores(query_block, key1, valid1, log_two), level_scores(query_block, key2, valid2, 2.0 * log_two), level_scores(query_block, pooled_k[2], valid3, 3.0 * log_two)], axis=2)
        value_rows = jnp.concatenate([val0, val1, val2, pooled_v[2]], 0)
        top = lax.optimization_barrier(jnp.max(scores, axis=2, keepdims=True))
        weights = jnp.exp(scores - top)
        total = lax.optimization_barrier(jnp.sum(weights, axis=2))
        rounded = weights.astype(jnp.bfloat16)
        summed = jnp.einsum('hqk,khd->hqd', rounded.astype(jnp.float32), value_rows.astype(jnp.float32))
        return (summed / total[..., None]).transpose(1, 0, 2).astype(jnp.bfloat16)
    blocks = lax.map(one_block, jnp.arange(length // quad, dtype=jnp.int32))
    return blocks.reshape(length, heads, width)
```

```python
import functools
import math

import jax
import jax.numpy as jnp
from jax import lax
from jax.experimental import pallas as pl
from jax.experimental.pallas import tpu as pltpu
from jax.sharding import PartitionSpec as P

BLOCK = 64
QUAD = 4 * BLOCK
HALF = 2 * BLOCK
NEAR = 5 * BLOCK
NEG = -1e30
F32 = jnp.float32
BF16 = jnp.bfloat16


def to_heads(values, scratch, heads):
    count, _, width = values.shape
    scratch[pl.ds(0, count * heads), :] = values.reshape(count * heads, width)
    return [scratch[pl.ds(h, count, stride=heads), :].astype(BF16) for h in range(heads)]


def halved(values):
    count, heads, width = values.shape
    pairs = values.reshape(count // 2, 2, heads, width)
    return pairs[:, 0] + pairs[:, 1]


def kernel(size, span, q_ref, k_ref, v_ref, o_ref,
           far, tail0, tailp, sendp, eq, e0, e1, e2, fk,
           bias, acc, top, total, tmp, otmp,
           t_send, t_recv, up_send, up_recv, pr_send, pr_recv):
    rows, heads, width = q_ref.shape
    own = rows // 8
    gain = math.log2(math.e) / math.sqrt(width)
    me = lax.axis_index("seq")
    col = lax.rem(me, 2)
    lev = me // 2
    levels = size // 2
    pair = me + 1 - 2 * col
    sources = (k_ref, v_ref)

    barrier = pltpu.get_barrier_semaphore()
    for step in (-2, -1, 1, 2):
        @pl.when((me + step >= 0) & (me + step < size))
        def _():
            pl.semaphore_signal(barrier, inc=1, device_id={"seq": me + step},
                                device_id_type=pl.DeviceIdType.MESH)

    def tail_copy(kv, part, target):
        if part == 0:
            src, dst = sources[kv].at[pl.ds(rows - BLOCK, BLOCK)], tail0.at[kv]
        else:
            src, dst = sendp.at[kv], tailp.at[kv]
        return pltpu.make_async_remote_copy(
            src_ref=src, dst_ref=dst, send_sem=t_send.at[kv, part], recv_sem=t_recv.at[kv, part],
            device_id={"seq": target}, device_id_type=pl.DeviceIdType.MESH)

    def up_copy(kv, b, target):
        return pltpu.make_async_remote_copy(
            src_ref=far.at[kv, b], dst_ref=far.at[kv, b],
            send_sem=up_send.at[kv, b], recv_sem=up_recv.at[kv, b],
            device_id={"seq": target}, device_id_type=pl.DeviceIdType.MESH)

    def pair_copy(kv, b):
        return pltpu.make_async_remote_copy(
            src_ref=far.at[kv, b], dst_ref=far.at[kv, b],
            send_sem=pr_send.at[kv, b], recv_sem=pr_recv.at[kv, b],
            device_id={"seq": pair}, device_id_type=pl.DeviceIdType.MESH)

    climbs = lev < levels - 1
    up = jnp.minimum(me + 2, size - 1)
    after = jnp.minimum(me + 1, size - 1)

    def split(kv, c):
        x = sources[kv][pl.ds(c * BLOCK, BLOCK)].astype(F32)
        two = halved(x)
        four = halved(two)
        eight = halved(four)
        two = two * 0.5
        four = four * 0.25
        far[kv, me, pl.ds(c * 8, 8)] = (eight * 0.125).astype(BF16)
        if c >= rows // BLOCK - 4 and c < rows // BLOCK - 1:
            sendp[kv, pl.ds(32 + 16 * (c - rows // BLOCK + 4), 16)] = four.astype(BF16)
        if c == rows // BLOCK - 2:
            sendp[kv, pl.ds(0, 32)] = two.astype(BF16)

    def spread(kv, c):
        x = sources[kv][pl.ds(c * BLOCK, BLOCK)].astype(F32)
        for h, part in enumerate(to_heads(x, tmp, heads)):
            e0[kv, h, pl.ds(BLOCK + c * BLOCK, BLOCK), :] = part
        if c < rows // BLOCK - 2:
            two = halved(x)
            for h, part in enumerate(to_heads(two * 0.5, tmp, heads)):
                e1[kv, h, pl.ds(BLOCK + c * 32, 32), :] = part
            if c < rows // BLOCK - 4:
                four = halved(two)
                for h, part in enumerate(to_heads(four * 0.25, tmp, heads)):
                    e2[kv, h, pl.ds(BLOCK + c * 16, 16), :] = part

    for kv in range(2):
        for c in range(rows // BLOCK):
            split(kv, c)

    lower = jnp.minimum(me, 2)
    upper = jnp.minimum(size - 1 - me, 2)
    pl.semaphore_wait(barrier, lower + upper)

    for kv in range(2):
        @pl.when(climbs)
        def _():
            up_copy(kv, me, up).start()

        @pl.when(me < size - 1)
        def _():
            tail_copy(kv, 0, after).start()
            tail_copy(kv, 1, after).start()

        @pl.when(col == 0)
        def _():
            pair_copy(kv, me).start()

    for kv in range(2):
        for c in range(rows // BLOCK):
            spread(kv, c)
    for c in range(rows // BLOCK):
        x = q_ref[pl.ds(c * BLOCK, BLOCK)].astype(F32)
        for h, part in enumerate(to_heads(x, tmp, heads)):
            eq[h, pl.ds(c * BLOCK, BLOCK), :] = part

    i = lax.broadcasted_iota(jnp.int32, (HALF, NEAR), 0)
    j = lax.broadcasted_iota(jnp.int32, (HALF, NEAR), 1)
    is0 = j < 192
    is2 = j >= 256
    level = jnp.where(is0, 0.0, jnp.where(is2, 2.0, 1.0))
    ok01 = jnp.where(is0, jnp.where((j <= i + BLOCK) & ((j >= BLOCK) | (i < BLOCK)), 1, 0),
                     jnp.where((j < 224) | (i >= BLOCK), 1, 0))
    for qd in range(rows // QUAD):
        for hf in range(2):
            ok = jnp.where(is2, jnp.where((j < 288) | (hf == 1), 1, 0), ok01)
            if qd == 0:
                real = (j >= BLOCK) & (j < 192) if hf == 0 else j < 256
                ok = jnp.where(real | (me > 0), ok, 0)
            bias[2 * qd + hf] = jnp.where(ok > 0, level, NEG)

    def near(qd):
        def body(h, _):
            for hf in range(2):
                at = qd * QUAD + hf * HALF
                q = eq[h, pl.ds(at, HALF), :]
                kk, vv = (jnp.concatenate([
                    e0[kv, h, pl.ds(at, 192), :],
                    e1[kv, h, pl.ds(at // 2, BLOCK), :],
                    e2[kv, h, pl.ds(qd * BLOCK, BLOCK), :]], 0) for kv in range(2))
                s = lax.dot_general(q, kk, (((1,), (1,)), ((), ())), preferred_element_type=F32)
                s = s * gain + bias[2 * qd + hf]
                m = jnp.max(s, axis=1, keepdims=True)
                w = jnp.exp2(s - m)
                total[h, pl.ds(at, HALF), :] = jnp.sum(w, axis=1, keepdims=True)
                top[h, pl.ds(at, HALF), :] = m
                acc[h, pl.ds(at, HALF), :] = jnp.dot(w.astype(BF16), vv, preferred_element_type=F32)
            return 0
        lax.fori_loop(0, heads, body, 0)

    for qd in range(1, rows // QUAD):
        near(qd)

    def pass_on(r, _):
        b = me - 2 * r
        for kv in range(2):
            up_copy(kv, b, up).wait_recv()

            @pl.when(climbs)
            def _():
                up_copy(kv, b, up).start()

            if kv == 0:
                pair_copy(kv, b).start()
            else:
                @pl.when(col == 1)
                def _():
                    pair_copy(kv, b).start()

        @pl.when(col == 1)
        def _():
            b = me + 1 - 2 * r

            @pl.when(r == 1)
            def _():
                pair_copy(1, b).wait_recv()

            @pl.when(r > 1)
            def _():
                up_copy(1, b, up).wait_recv()

            @pl.when(climbs)
            def _():
                up_copy(1, b, up).start()
        return 0

    def last_even():
        @pl.when(col == 1)
        def _():
            b = me - 1 - 2 * lev

            @pl.when(lev == 0)
            def _():
                pair_copy(1, b).wait_recv()

            @pl.when(lev > 0)
            def _():
                up_copy(1, b, up).wait_recv()

            @pl.when(climbs)
            def _():
                up_copy(1, b, up).start()

    lax.fori_loop(1, lev + 1, pass_on, 0)
    last_even()

    @pl.when(me == 0)
    def _():
        for kv in range(2):
            for h in range(heads):
                e0[kv, h, pl.ds(0, BLOCK), :] = jnp.zeros((BLOCK, width), BF16)
                e1[kv, h, pl.ds(0, BLOCK), :] = jnp.zeros((BLOCK, width), BF16)
                e2[kv, h, pl.ds(0, BLOCK), :] = jnp.zeros((BLOCK, width), BF16)

    @pl.when(me > 0)
    def _():
        for kv in range(2):
            tail_copy(kv, 0, after).wait_recv()
            tail_copy(kv, 1, after).wait_recv()
            x = tail0[kv].astype(F32)
            for h, part in enumerate(to_heads(x, tmp, heads)):
                e0[kv, h, pl.ds(0, BLOCK), :] = part
            two = halved(x)
            four = halved(two)
            for h, part in enumerate(to_heads(two * 0.5, tmp, heads)):
                e1[kv, h, pl.ds(32, 32), :] = part
            for h, part in enumerate(to_heads(four * 0.25, tmp, heads)):
                e2[kv, h, pl.ds(48, 16), :] = part
            y = tailp[kv].astype(F32)
            for h, part in enumerate(to_heads(y, tmp, heads)):
                e1[kv, h, pl.ds(0, 32), :] = part[:32]
                e2[kv, h, pl.ds(0, 48), :] = part[32:]

    near(0)

    def from_pair(r, _):
        b = me - 1 - 2 * r

        @pl.when(col == 0)
        def _():
            pair_copy(0, b).wait_recv()
            pair_copy(1, b).wait_recv()

        @pl.when(col == 1)
        def _():
            pair_copy(0, b).wait_recv()
        return 0

    lax.fori_loop(0, lev + col, from_pair, 0)

    def arrange(b, _):
        for kv in range(2):
            @pl.when(b < me)
            def _():
                x = far[kv, b].astype(F32)
                for h, part in enumerate(to_heads(x, tmp, heads)):
                    fk[kv, h, pl.ds(pl.multiple_of(b * own, own), own), :] = part

            @pl.when(b >= me)
            def _():
                for h in range(heads):
                    fk[kv, h, pl.ds(pl.multiple_of(b * own, own), own), :] = jnp.zeros((own, width), BF16)
        return 0

    chunks = (me + span - 1) // span
    lax.fori_loop(0, chunks * span, arrange, 0)
    wide = span * own

    def finish(h, _):
        for qd in range(rows // QUAD):
            limit = own * me + 32 * (qd - 1)
            for hf in range(2):
                at = qd * QUAD + hf * HALF
                q = eq[h, pl.ds(at, HALF), :]

                def chunk(c, state):
                    m, l, a = state
                    start = pl.multiple_of(c * wide, wide)
                    place = start + lax.broadcasted_iota(jnp.int32, (1, wide), 1)
                    s = lax.dot_general(q, fk[0, h, pl.ds(start, wide), :], (((1,), (1,)), ((), ())),
                                        preferred_element_type=F32)
                    s = s * gain + jnp.where(place < limit, 3.0, NEG)
                    fresh = jnp.maximum(m, jnp.max(s, axis=1, keepdims=True))
                    fade = jnp.exp2(m - fresh)
                    w = jnp.exp2(s - fresh)
                    l = l * fade + jnp.sum(w, axis=1, keepdims=True)
                    a = a * fade + jnp.dot(w.astype(BF16), fk[1, h, pl.ds(start, wide), :],
                                           preferred_element_type=F32)
                    return (fresh, l, a)

                state = (top[h, pl.ds(at, HALF), :], total[h, pl.ds(at, HALF), :],
                         acc[h, pl.ds(at, HALF), :])
                m, l, a = lax.fori_loop(0, chunks, chunk, state)
                acc[h, pl.ds(at, HALF), :] = a / l
        return 0

    lax.fori_loop(0, heads, finish, 0)
    for c in range(rows // HALF):
        for h in range(heads):
            otmp[pl.ds(h, HALF, stride=heads), :] = acc[h, pl.ds(c * HALF, HALF), :]
        o_ref[pl.ds(c * HALF, HALF)] = otmp[...].reshape(HALF, heads, width).astype(BF16)

    @pl.when(me < size - 1)
    def _():
        for kv in range(2):
            tail_copy(kv, 0, after).wait_send()
            tail_copy(kv, 1, after).wait_send()

    @pl.when(col == 0)
    def _():
        for kv in range(2):
            pair_copy(kv, me).wait_send()

    def sent(r, _):
        b = me - 2 * r

        @pl.when(climbs)
        def _():
            for kv in range(2):
                up_copy(kv, b, up).wait_send()

            @pl.when(col == 1)
            def _():
                up_copy(1, b - 1, up).wait_send()

        @pl.when(r > 0)
        def _():
            pair_copy(0, b).wait_send()

            @pl.when(col == 1)
            def _():
                pair_copy(1, b).wait_send()
        return 0

    lax.fori_loop(0, lev + 1, sent, 0)


def shards(size, queries, keys, values):
    rows, heads, width = queries.shape
    own = rows // 8
    span = max(n for n in range(1, min(size, 8) + 1) if size % n == 0)
    vmem = pl.BlockSpec(memory_space=pltpu.VMEM)
    return pl.pallas_call(
        functools.partial(kernel, size, span),
        out_shape=jax.ShapeDtypeStruct((rows, heads, width), BF16),
        in_specs=[vmem] * 3,
        out_specs=vmem,
        scratch_shapes=[
            pltpu.VMEM((2, size, own, heads, width), BF16),
            pltpu.VMEM((2, BLOCK, heads, width), BF16),
            pltpu.VMEM((2, 80, heads, width), BF16),
            pltpu.VMEM((2, 80, heads, width), BF16),
            pltpu.VMEM((heads, rows, width), BF16),
            pltpu.VMEM((2, heads, rows + BLOCK, width), BF16),
            pltpu.VMEM((2, heads, rows // 2, width), BF16),
            pltpu.VMEM((2, heads, rows // 4, width), BF16),
            pltpu.VMEM((2, heads, size * own, width), BF16),
            pltpu.VMEM((rows // HALF, HALF, NEAR), F32),
            pltpu.VMEM((heads, rows, width), F32),
            pltpu.VMEM((heads, rows, 1), F32),
            pltpu.VMEM((heads, rows, 1), F32),
            pltpu.VMEM((80 * heads, width), F32),
            pltpu.VMEM((HALF * heads, width), F32),
            pltpu.SemaphoreType.DMA((2, 2)),
            pltpu.SemaphoreType.DMA((2, 2)),
            pltpu.SemaphoreType.DMA((2, size)),
            pltpu.SemaphoreType.DMA((2, size)),
            pltpu.SemaphoreType.DMA((2, size)),
            pltpu.SemaphoreType.DMA((2, size)),
        ],
        compiler_params=pltpu.CompilerParams(
            collective_id=0, has_side_effects=True, vmem_limit_bytes=60 * 2**20),
    )(queries, keys, values)


def solution(mesh):
    spec = P(("groups", "seq"), "heads", None)
    return jax.shard_map(
        functools.partial(shards, mesh.shape["seq"]),
        mesh=mesh, in_specs=(spec,) * 3, out_specs=spec, check_vma=False)
```

```python
import functools
import math

import jax
import jax.numpy as jnp
from jax import lax
from jax.experimental import pallas as pl
from jax.experimental.pallas import tpu as pltpu
from jax.sharding import PartitionSpec as P

BLOCK = 64
QUAD = 4 * BLOCK
HALF = 2 * BLOCK
NEAR = 5 * BLOCK
NEG = -1e30
F32 = jnp.float32
BF16 = jnp.bfloat16


def to_heads(values, scratch, heads):
    count, _, width = values.shape
    scratch[pl.ds(0, count * heads), :] = values.reshape(count * heads, width)
    return [scratch[pl.ds(h, count, stride=heads), :].astype(BF16) for h in range(heads)]


def halved(values):
    count, heads, width = values.shape
    pairs = values.reshape(count // 2, 2, heads, width)
    return pairs[:, 0] + pairs[:, 1]


def kernel(size, span, q_ref, k_ref, v_ref, o_ref,
           far, tail0, tailp, sendp, eq, e0, e1, e2, fk,
           bias, acc, top, total, tmp, otmp,
           t_send, t_recv, up_send, up_recv, pr_send, pr_recv):
    rows, heads, width = q_ref.shape
    own = rows // 8
    gain = math.log2(math.e) / math.sqrt(width)
    me = lax.axis_index("seq")
    col = lax.rem(me, 2)
    lev = me // 2
    levels = size // 2
    together = 2 - heads % 2
    pair = me + 1 - 2 * col
    sources = (k_ref, v_ref)

    barrier = pltpu.get_barrier_semaphore()
    for step in (-2, -1, 1, 2):
        @pl.when((me + step >= 0) & (me + step < size))
        def _():
            pl.semaphore_signal(barrier, inc=1, device_id={"seq": me + step},
                                device_id_type=pl.DeviceIdType.MESH)

    def tail_copy(kv, part, target):
        if part == 0:
            src, dst = sources[kv].at[pl.ds(rows - BLOCK, BLOCK)], tail0.at[kv]
        else:
            src, dst = sendp.at[kv], tailp.at[kv]
        return pltpu.make_async_remote_copy(
            src_ref=src, dst_ref=dst, send_sem=t_send.at[kv, part], recv_sem=t_recv.at[kv, part],
            device_id={"seq": target}, device_id_type=pl.DeviceIdType.MESH)

    def up_copy(kv, b, target):
        return pltpu.make_async_remote_copy(
            src_ref=far.at[kv, b], dst_ref=far.at[kv, b],
            send_sem=up_send.at[kv, b], recv_sem=up_recv.at[kv, b],
            device_id={"seq": target}, device_id_type=pl.DeviceIdType.MESH)

    def pair_copy(kv, b):
        return pltpu.make_async_remote_copy(
            src_ref=far.at[kv, b], dst_ref=far.at[kv, b],
            send_sem=pr_send.at[kv, b], recv_sem=pr_recv.at[kv, b],
            device_id={"seq": pair}, device_id_type=pl.DeviceIdType.MESH)

    climbs = lev < levels - 1
    up = jnp.minimum(me + 2, size - 1)
    after = jnp.minimum(me + 1, size - 1)

    def split(kv, c):
        x = sources[kv][pl.ds(c * BLOCK, BLOCK)].astype(F32)
        two = halved(x)
        four = halved(two)
        eight = halved(four)
        two = two * 0.5
        four = four * 0.25
        far[kv, me, pl.ds(c * 8, 8)] = (eight * 0.125).astype(BF16)
        if c >= rows // BLOCK - 4 and c < rows // BLOCK - 1:
            sendp[kv, pl.ds(32 + 16 * (c - rows // BLOCK + 4), 16)] = four.astype(BF16)
        if c == rows // BLOCK - 2:
            sendp[kv, pl.ds(0, 32)] = two.astype(BF16)

    def spread(kv, c):
        x = sources[kv][pl.ds(c * BLOCK, BLOCK)].astype(F32)
        for h, part in enumerate(to_heads(x, tmp, heads)):
            e0[kv, h, pl.ds(BLOCK + c * BLOCK, BLOCK), :] = part
        if c < rows // BLOCK - 2:
            two = halved(x)
            for h, part in enumerate(to_heads(two * 0.5, tmp, heads)):
                e1[kv, h, pl.ds(BLOCK + c * 32, 32), :] = part
            if c < rows // BLOCK - 4:
                four = halved(two)
                for h, part in enumerate(to_heads(four * 0.25, tmp, heads)):
                    e2[kv, h, pl.ds(BLOCK + c * 16, 16), :] = part

    for kv in (1, 0):
        for c in range(rows // BLOCK):
            split(kv, c)

    lower = jnp.minimum(me, 2)
    upper = jnp.minimum(size - 1 - me, 2)
    pl.semaphore_wait(barrier, lower + upper)

    for kv in (1, 0):
        @pl.when(climbs)
        def _():
            up_copy(kv, me, up).start()

        @pl.when(col == 0)
        def _():
            pair_copy(kv, me).start()

    @pl.when(me < size - 1)
    def _():
        for kv in range(2):
            tail_copy(kv, 0, after).start()
            tail_copy(kv, 1, after).start()

    for kv in range(2):
        for c in range(rows // BLOCK):
            spread(kv, c)
    for c in range(rows // BLOCK):
        x = q_ref[pl.ds(c * BLOCK, BLOCK)].astype(F32)
        for h, part in enumerate(to_heads(x, tmp, heads)):
            eq[h, pl.ds(c * BLOCK, BLOCK), :] = part

    i = lax.broadcasted_iota(jnp.int32, (HALF, NEAR), 0)
    j = lax.broadcasted_iota(jnp.int32, (HALF, NEAR), 1)
    is0 = j < 192
    is2 = j >= 256
    level = jnp.where(is0, 0.0, jnp.where(is2, 2.0, 1.0))
    ok01 = jnp.where(is0, jnp.where((j <= i + BLOCK) & ((j >= BLOCK) | (i < BLOCK)), 1, 0),
                     jnp.where((j < 224) | (i >= BLOCK), 1, 0))
    for qd in range(rows // QUAD):
        for hf in range(2):
            ok = jnp.where(is2, jnp.where((j < 288) | (hf == 1), 1, 0), ok01)
            if qd == 0:
                real = (j >= BLOCK) & (j < 192) if hf == 0 else j < 256
                ok = jnp.where(real | (me > 0), ok, 0)
            bias[2 * qd + hf] = jnp.where(ok > 0, level, NEG)

    def near(qd):
        def body(g, _):
            for part in range(2 * together):
                h, hf = g * together + part // 2, part % 2
                at = qd * QUAD + hf * HALF
                q = eq[h, pl.ds(at, HALF), :]
                kk, vv = (jnp.concatenate([
                    e0[kv, h, pl.ds(at, 192), :],
                    e1[kv, h, pl.ds(at // 2, BLOCK), :],
                    e2[kv, h, pl.ds(qd * BLOCK, BLOCK), :]], 0) for kv in range(2))
                s = lax.dot_general(q, kk, (((1,), (1,)), ((), ())), preferred_element_type=F32)
                s = s * gain + bias[2 * qd + hf]
                m = jnp.max(s, axis=1, keepdims=True)
                w = jnp.exp2(s - m)
                total[h, pl.ds(at, HALF), :] = jnp.sum(w, axis=1, keepdims=True)
                top[h, pl.ds(at, HALF), :] = m
                acc[h, pl.ds(at, HALF), :] = jnp.dot(w.astype(BF16), vv, preferred_element_type=F32)
            return 0
        lax.fori_loop(0, heads // together, body, 0)

    for qd in range(1, rows // QUAD):
        near(qd)

    def pass_on(r, _):
        b = me - 2 * r
        for kv in range(2):
            up_copy(kv, b, up).wait_recv()

            @pl.when(climbs)
            def _():
                up_copy(kv, b, up).start()

            if kv == 0:
                pair_copy(kv, b).start()
            else:
                @pl.when(col == 1)
                def _():
                    pair_copy(kv, b).start()

        @pl.when((col == 1) & climbs)
        def _():
            even_on(r)
        return 0

    def even_on(r):
        b = me + 1 - 2 * r

        @pl.when(r == 1)
        def _():
            pair_copy(1, b).wait_recv()

        @pl.when(r > 1)
        def _():
            up_copy(1, b, up).wait_recv()

        up_copy(1, b, up).start()

    lax.fori_loop(1, lev + 1, pass_on, 0)

    @pl.when((col == 1) & climbs)
    def _():
        even_on(lev + 1)

    @pl.when(me == 0)
    def _():
        for kv in range(2):
            for h in range(heads):
                e0[kv, h, pl.ds(0, BLOCK), :] = jnp.zeros((BLOCK, width), BF16)
                e1[kv, h, pl.ds(0, BLOCK), :] = jnp.zeros((BLOCK, width), BF16)
                e2[kv, h, pl.ds(0, BLOCK), :] = jnp.zeros((BLOCK, width), BF16)

    @pl.when(me > 0)
    def _():
        for kv in range(2):
            tail_copy(kv, 0, after).wait_recv()
            tail_copy(kv, 1, after).wait_recv()
            x = tail0[kv].astype(F32)
            for h, part in enumerate(to_heads(x, tmp, heads)):
                e0[kv, h, pl.ds(0, BLOCK), :] = part
            two = halved(x)
            four = halved(two)
            for h, part in enumerate(to_heads(two * 0.5, tmp, heads)):
                e1[kv, h, pl.ds(32, 32), :] = part
            for h, part in enumerate(to_heads(four * 0.25, tmp, heads)):
                e2[kv, h, pl.ds(48, 16), :] = part
            y = tailp[kv].astype(F32)
            for h, part in enumerate(to_heads(y, tmp, heads)):
                e1[kv, h, pl.ds(0, 32), :] = part[:32]
                e2[kv, h, pl.ds(0, 48), :] = part[32:]

    near(0)

    def arrange(s, _):
        b = me - 1 - s
        place = pl.multiple_of(s * own, own)
        even = lax.rem(s, 2) == 0

        @pl.when((s < me) & even)
        def _():
            pair_copy(0, b).wait_recv()

            @pl.when(col == 0)
            def _():
                pair_copy(1, b).wait_recv()

            @pl.when((col == 1) & jnp.logical_not(climbs) & (s == 0))
            def _():
                pair_copy(1, b).wait_recv()

            @pl.when((col == 1) & jnp.logical_not(climbs) & (s > 0))
            def _():
                up_copy(1, b, up).wait_recv()

        @pl.when(s < me)
        def _():
            for kv in range(2):
                x = far[kv, b].astype(F32)
                for h, part in enumerate(to_heads(x, tmp, heads)):
                    fk[kv, h, pl.ds(place, own), :] = part

        @pl.when(s >= me)
        def _():
            for kv in range(2):
                for h in range(heads):
                    fk[kv, h, pl.ds(place, own), :] = jnp.zeros((own, width), BF16)
        return 0

    wide = span * own

    def chunk(c, _):
        lax.fori_loop(c * span, (c + 1) * span, arrange, 0)
        start = pl.multiple_of(c * wide, wide)
        place = start + lax.broadcasted_iota(jnp.int32, (1, wide), 1)
        known = jnp.where(place < own * me, 3.0, NEG)
        masks = [jnp.where((place >= own // 2) & (place < own), NEG, known), known]

        def body(h, _):
            for qd in range(rows // QUAD):
                for hf in range(2):
                    at = qd * QUAD + hf * HALF
                    m = top[h, pl.ds(at, HALF), :]
                    s = lax.dot_general(eq[h, pl.ds(at, HALF), :], fk[0, h, pl.ds(start, wide), :],
                                        (((1,), (1,)), ((), ())), preferred_element_type=F32)
                    s = s * gain + masks[min(qd, 1)]
                    fresh = jnp.maximum(m, jnp.max(s, axis=1, keepdims=True))
                    fade = jnp.exp2(m - fresh)
                    w = jnp.exp2(s - fresh)
                    top[h, pl.ds(at, HALF), :] = fresh
                    total[h, pl.ds(at, HALF), :] = (
                        total[h, pl.ds(at, HALF), :] * fade + jnp.sum(w, axis=1, keepdims=True))
                    acc[h, pl.ds(at, HALF), :] = acc[h, pl.ds(at, HALF), :] * fade + jnp.dot(
                        w.astype(BF16), fk[1, h, pl.ds(start, wide), :], preferred_element_type=F32)
            return 0

        lax.fori_loop(0, heads, body, 0)
        return 0

    lax.fori_loop(0, (me + span - 1) // span, chunk, 0)
    for c in range(rows // HALF):
        for h in range(heads):
            otmp[pl.ds(h, HALF, stride=heads), :] = (
                acc[h, pl.ds(c * HALF, HALF), :] / total[h, pl.ds(c * HALF, HALF), :])
        o_ref[pl.ds(c * HALF, HALF)] = otmp[...].reshape(HALF, heads, width).astype(BF16)

    @pl.when(me < size - 1)
    def _():
        for kv in range(2):
            tail_copy(kv, 0, after).wait_send()
            tail_copy(kv, 1, after).wait_send()

    @pl.when(col == 0)
    def _():
        for kv in range(2):
            pair_copy(kv, me).wait_send()

    def sent(r, _):
        b = me - 2 * r

        @pl.when(climbs)
        def _():
            for kv in range(2):
                up_copy(kv, b, up).wait_send()

            @pl.when(col == 1)
            def _():
                up_copy(1, b - 1, up).wait_send()

        @pl.when(r > 0)
        def _():
            pair_copy(0, b).wait_send()

            @pl.when(col == 1)
            def _():
                pair_copy(1, b).wait_send()
        return 0

    lax.fori_loop(0, lev + 1, sent, 0)


def shards(size, queries, keys, values):
    rows, heads, width = queries.shape
    own = rows // 8
    span = max(n for n in range(1, min(size, 4) + 1) if size % n == 0)
    vmem = pl.BlockSpec(memory_space=pltpu.VMEM)
    return pl.pallas_call(
        functools.partial(kernel, size, span),
        out_shape=jax.ShapeDtypeStruct((rows, heads, width), BF16),
        in_specs=[vmem] * 3,
        out_specs=vmem,
        scratch_shapes=[
            pltpu.VMEM((2, size, own, heads, width), BF16),
            pltpu.VMEM((2, BLOCK, heads, width), BF16),
            pltpu.VMEM((2, 80, heads, width), BF16),
            pltpu.VMEM((2, 80, heads, width), BF16),
            pltpu.VMEM((heads, rows, width), BF16),
            pltpu.VMEM((2, heads, rows + BLOCK, width), BF16),
            pltpu.VMEM((2, heads, rows // 2, width), BF16),
            pltpu.VMEM((2, heads, rows // 4, width), BF16),
            pltpu.VMEM((2, heads, size * own, width), BF16),
            pltpu.VMEM((rows // HALF, HALF, NEAR), F32),
            pltpu.VMEM((heads, rows, width), F32),
            pltpu.VMEM((heads, rows, 1), F32),
            pltpu.VMEM((heads, rows, 1), F32),
            pltpu.VMEM((80 * heads, width), F32),
            pltpu.VMEM((HALF * heads, width), F32),
            pltpu.SemaphoreType.DMA((2, 2)),
            pltpu.SemaphoreType.DMA((2, 2)),
            pltpu.SemaphoreType.DMA((2, size)),
            pltpu.SemaphoreType.DMA((2, size)),
            pltpu.SemaphoreType.DMA((2, size)),
            pltpu.SemaphoreType.DMA((2, size)),
        ],
        compiler_params=pltpu.CompilerParams(
            collective_id=0, has_side_effects=True, vmem_limit_bytes=60 * 2**20),
    )(queries, keys, values)


def solution(mesh):
    spec = P(("groups", "seq"), "heads", None)
    return jax.shard_map(
        functools.partial(shards, mesh.shape["seq"]),
        mesh=mesh, in_specs=(spec,) * 3, out_specs=spec, check_vma=False)
```

```python
import functools
import math

import jax
import jax.numpy as jnp
from jax import lax
from jax.experimental import pallas as pl
from jax.experimental.pallas import tpu as pltpu
from jax.sharding import PartitionSpec as P

BLOCK = 64
QUAD = 4 * BLOCK
HALF = 2 * BLOCK
NEAR = 5 * BLOCK
NEG = -1e30
F32 = jnp.float32
BF16 = jnp.bfloat16


def to_heads(values, scratch, heads):
    count, _, width = values.shape
    scratch[pl.ds(0, count * heads), :] = values.reshape(count * heads, width)
    return [scratch[pl.ds(h, count, stride=heads), :].astype(BF16) for h in range(heads)]


def halved(values):
    count, heads, width = values.shape
    pairs = values.reshape(count // 2, 2, heads, width)
    return pairs[:, 0] + pairs[:, 1]


def across(column, count):
    width = column.shape[1]
    parts = [column] * (count // width)
    if count % width:
        parts.append(column[:, :count % width])
    return jnp.concatenate(parts, 1) if len(parts) > 1 else parts[0]


def with_ones(values):
    return jnp.concatenate([values, jnp.ones_like(values)], 1)


def kernel(size, span, q_ref, k_ref, v_ref, o_ref,
           far, tail0, tailp, sendp, eq, e0, e1, e2, fk,
           bias, acc, top, total, tmp, otmp,
           t_send, t_recv, up_send, up_recv, pr_send, pr_recv):
    rows, heads, width = q_ref.shape
    own = rows // 8
    gain = math.log2(math.e) / math.sqrt(width)
    me = lax.axis_index("seq")
    col = lax.rem(me, 2)
    lev = me // 2
    levels = size // 2
    together = 2 - heads % 2
    pair = me + 1 - 2 * col
    sources = (k_ref, v_ref)

    barrier = pltpu.get_barrier_semaphore()
    for step in (-2, -1, 1, 2):
        @pl.when((me + step >= 0) & (me + step < size))
        def _():
            pl.semaphore_signal(barrier, inc=1, device_id={"seq": me + step},
                                device_id_type=pl.DeviceIdType.MESH)

    def tail_copy(kv, part, target):
        if part == 0:
            src, dst = sources[kv].at[pl.ds(rows - BLOCK, BLOCK)], tail0.at[kv]
        else:
            src, dst = sendp.at[kv], tailp.at[kv]
        return pltpu.make_async_remote_copy(
            src_ref=src, dst_ref=dst, send_sem=t_send.at[kv, part], recv_sem=t_recv.at[kv, part],
            device_id={"seq": target}, device_id_type=pl.DeviceIdType.MESH)

    def up_copy(kv, b, target):
        return pltpu.make_async_remote_copy(
            src_ref=far.at[kv, b], dst_ref=far.at[kv, b],
            send_sem=up_send.at[kv, b], recv_sem=up_recv.at[kv, b],
            device_id={"seq": target}, device_id_type=pl.DeviceIdType.MESH)

    def pair_copy(kv, b):
        return pltpu.make_async_remote_copy(
            src_ref=far.at[kv, b], dst_ref=far.at[kv, b],
            send_sem=pr_send.at[kv, b], recv_sem=pr_recv.at[kv, b],
            device_id={"seq": pair}, device_id_type=pl.DeviceIdType.MESH)

    climbs = lev < levels - 1
    up = jnp.minimum(me + 2, size - 1)
    after = jnp.minimum(me + 1, size - 1)

    def split(kv, c):
        x = sources[kv][pl.ds(c * BLOCK, BLOCK)].astype(F32)
        two = halved(x)
        four = halved(two)
        eight = halved(four)
        two = two * 0.5
        four = four * 0.25
        far[kv, me, pl.ds(c * 8, 8)] = (eight * 0.125).astype(BF16)
        if c >= rows // BLOCK - 4 and c < rows // BLOCK - 1:
            sendp[kv, pl.ds(32 + 16 * (c - rows // BLOCK + 4), 16)] = four.astype(BF16)
        if c == rows // BLOCK - 2:
            sendp[kv, pl.ds(0, 32)] = two.astype(BF16)

    def spread(kv, c):
        x = sources[kv][pl.ds(c * BLOCK, BLOCK)].astype(F32)
        for h, part in enumerate(to_heads(x, tmp, heads)):
            e0[kv, h, pl.ds(BLOCK + c * BLOCK, BLOCK), :] = part
        if c < rows // BLOCK - 2:
            two = halved(x)
            for h, part in enumerate(to_heads(two * 0.5, tmp, heads)):
                e1[kv, h, pl.ds(BLOCK + c * 32, 32), :] = part
            if c < rows // BLOCK - 4:
                four = halved(two)
                for h, part in enumerate(to_heads(four * 0.25, tmp, heads)):
                    e2[kv, h, pl.ds(BLOCK + c * 16, 16), :] = part

    for kv in (1, 0):
        for c in range(rows // BLOCK):
            split(kv, c)

    lower = jnp.minimum(me, 2)
    upper = jnp.minimum(size - 1 - me, 2)
    pl.semaphore_wait(barrier, lower + upper)

    for kv in (1, 0):
        @pl.when(climbs)
        def _():
            up_copy(kv, me, up).start()

        @pl.when(col == 0)
        def _():
            pair_copy(kv, me).start()

    @pl.when(me < size - 1)
    def _():
        for kv in range(2):
            tail_copy(kv, 0, after).start()
            tail_copy(kv, 1, after).start()

    for kv in range(2):
        for c in range(rows // BLOCK):
            spread(kv, c)
    for c in range(rows // BLOCK):
        x = q_ref[pl.ds(c * BLOCK, BLOCK)].astype(F32)
        for h, part in enumerate(to_heads(x, tmp, heads)):
            eq[h, pl.ds(c * BLOCK, BLOCK), :] = part

    i = lax.broadcasted_iota(jnp.int32, (HALF, NEAR), 0)
    j = lax.broadcasted_iota(jnp.int32, (HALF, NEAR), 1)
    is0 = j < 192
    is2 = j >= 256
    level = jnp.where(is0, 0.0, jnp.where(is2, 2.0, 1.0))
    ok01 = jnp.where(is0, jnp.where((j <= i + BLOCK) & ((j >= BLOCK) | (i < BLOCK)), 1, 0),
                     jnp.where((j < 224) | (i >= BLOCK), 1, 0))
    for qd in range(rows // QUAD):
        for hf in range(2):
            ok = jnp.where(is2, jnp.where((j < 288) | (hf == 1), 1, 0), ok01)
            if qd == 0:
                real = (j >= BLOCK) & (j < 192) if hf == 0 else j < 256
                ok = jnp.where(real | (me > 0), ok, 0)
            bias[2 * qd + hf] = jnp.where(ok > 0, level, NEG)

    def near(qd):
        def body(g, _):
            for part in range(2 * together):
                h, hf = g * together + part // 2, part % 2
                at = qd * QUAD + hf * HALF
                q = eq[h, pl.ds(at, HALF), :]
                kk, vv = (jnp.concatenate([
                    e0[kv, h, pl.ds(at, 192), :],
                    e1[kv, h, pl.ds(at // 2, BLOCK), :],
                    e2[kv, h, pl.ds(qd * BLOCK, BLOCK), :]], 0) for kv in range(2))
                s = lax.dot_general(q, kk, (((1,), (1,)), ((), ())), preferred_element_type=F32)
                s = s * gain + bias[2 * qd + hf]
                m = jnp.broadcast_to(jnp.max(s, axis=1, keepdims=True), (HALF, width))
                w = jnp.exp2(s - across(m, NEAR)).astype(BF16)
                both = jnp.dot(w, with_ones(vv), preferred_element_type=F32)
                top[h, pl.ds(at, HALF), :] = m
                acc[h, pl.ds(at, HALF), :] = both[:, :width]
                total[h, pl.ds(at, HALF), :] = both[:, width:]
            return 0
        lax.fori_loop(0, heads // together, body, 0)

    for qd in range(1, rows // QUAD):
        near(qd)

    def pass_on(r, _):
        b = me - 2 * r
        for kv in range(2):
            up_copy(kv, b, up).wait_recv()

            @pl.when(climbs)
            def _():
                up_copy(kv, b, up).start()

            if kv == 0:
                pair_copy(kv, b).start()
            else:
                @pl.when(col == 1)
                def _():
                    pair_copy(kv, b).start()

        @pl.when((col == 1) & climbs)
        def _():
            even_on(r)
        return 0

    def even_on(r):
        b = me + 1 - 2 * r

        @pl.when(r == 1)
        def _():
            pair_copy(1, b).wait_recv()

        @pl.when(r > 1)
        def _():
            up_copy(1, b, up).wait_recv()

        up_copy(1, b, up).start()

    lax.fori_loop(1, lev + 1, pass_on, 0)

    @pl.when((col == 1) & climbs)
    def _():
        even_on(lev + 1)

    @pl.when(me == 0)
    def _():
        for kv in range(2):
            for h in range(heads):
                e0[kv, h, pl.ds(0, BLOCK), :] = jnp.zeros((BLOCK, width), BF16)
                e1[kv, h, pl.ds(0, BLOCK), :] = jnp.zeros((BLOCK, width), BF16)
                e2[kv, h, pl.ds(0, BLOCK), :] = jnp.zeros((BLOCK, width), BF16)

    @pl.when(me > 0)
    def _():
        for kv in range(2):
            tail_copy(kv, 0, after).wait_recv()
            tail_copy(kv, 1, after).wait_recv()
            x = tail0[kv].astype(F32)
            for h, part in enumerate(to_heads(x, tmp, heads)):
                e0[kv, h, pl.ds(0, BLOCK), :] = part
            two = halved(x)
            four = halved(two)
            for h, part in enumerate(to_heads(two * 0.5, tmp, heads)):
                e1[kv, h, pl.ds(32, 32), :] = part
            for h, part in enumerate(to_heads(four * 0.25, tmp, heads)):
                e2[kv, h, pl.ds(48, 16), :] = part
            y = tailp[kv].astype(F32)
            for h, part in enumerate(to_heads(y, tmp, heads)):
                e1[kv, h, pl.ds(0, 32), :] = part[:32]
                e2[kv, h, pl.ds(0, 48), :] = part[32:]

    near(0)

    def arrange(s, _):
        b = me - 1 - s
        place = pl.multiple_of(s * own, own)
        even = lax.rem(s, 2) == 0

        @pl.when((s < me) & even)
        def _():
            pair_copy(0, b).wait_recv()

            @pl.when(col == 0)
            def _():
                pair_copy(1, b).wait_recv()

            @pl.when((col == 1) & jnp.logical_not(climbs) & (s == 0))
            def _():
                pair_copy(1, b).wait_recv()

            @pl.when((col == 1) & jnp.logical_not(climbs) & (s > 0))
            def _():
                up_copy(1, b, up).wait_recv()

        @pl.when(s < me)
        def _():
            for kv in range(2):
                x = far[kv, b].astype(F32)
                for h, part in enumerate(to_heads(x, tmp, heads)):
                    fk[kv, h, pl.ds(place, own), :] = part

        @pl.when(s >= me)
        def _():
            for kv in range(2):
                for h in range(heads):
                    fk[kv, h, pl.ds(place, own), :] = jnp.zeros((own, width), BF16)
        return 0

    wide = span * own

    def chunk(c, _):
        lax.fori_loop(c * span, (c + 1) * span, arrange, 0)
        start = pl.multiple_of(c * wide, wide)
        place = start + lax.broadcasted_iota(jnp.int32, (1, wide), 1)
        known = jnp.where(place < own * me, 3.0, NEG)
        masks = [jnp.where((place >= own // 2) & (place < own), NEG, known), known]

        def body(h, _):
            for qd in range(rows // QUAD):
                for hf in range(2):
                    at = qd * QUAD + hf * HALF
                    m = top[h, pl.ds(at, HALF), :]
                    s = lax.dot_general(eq[h, pl.ds(at, HALF), :], fk[0, h, pl.ds(start, wide), :],
                                        (((1,), (1,)), ((), ())), preferred_element_type=F32)
                    s = s * gain + masks[min(qd, 1)]
                    fresh = jnp.maximum(m, jnp.max(s, axis=1, keepdims=True))
                    fade = jnp.exp2(m - fresh)
                    w = jnp.exp2(s - across(fresh, wide)).astype(BF16)
                    both = jnp.dot(w, with_ones(fk[1, h, pl.ds(start, wide), :]),
                                   preferred_element_type=F32)
                    top[h, pl.ds(at, HALF), :] = fresh
                    acc[h, pl.ds(at, HALF), :] = acc[h, pl.ds(at, HALF), :] * fade + both[:, :width]
                    total[h, pl.ds(at, HALF), :] = (
                        total[h, pl.ds(at, HALF), :] * fade + both[:, width:])
            return 0

        lax.fori_loop(0, heads, body, 0)
        return 0

    lax.fori_loop(0, (me + span - 1) // span, chunk, 0)
    for c in range(rows // HALF):
        for h in range(heads):
            otmp[pl.ds(h, HALF, stride=heads), :] = (
                acc[h, pl.ds(c * HALF, HALF), :] / total[h, pl.ds(c * HALF, HALF), :])
        o_ref[pl.ds(c * HALF, HALF)] = otmp[...].reshape(HALF, heads, width).astype(BF16)

    @pl.when(me < size - 1)
    def _():
        for kv in range(2):
            tail_copy(kv, 0, after).wait_send()
            tail_copy(kv, 1, after).wait_send()

    @pl.when(col == 0)
    def _():
        for kv in range(2):
            pair_copy(kv, me).wait_send()

    def sent(r, _):
        b = me - 2 * r

        @pl.when(climbs)
        def _():
            for kv in range(2):
                up_copy(kv, b, up).wait_send()

            @pl.when(col == 1)
            def _():
                up_copy(1, b - 1, up).wait_send()

        @pl.when(r > 0)
        def _():
            pair_copy(0, b).wait_send()

            @pl.when(col == 1)
            def _():
                pair_copy(1, b).wait_send()
        return 0

    lax.fori_loop(0, lev + 1, sent, 0)


def shards(size, queries, keys, values):
    rows, heads, width = queries.shape
    own = rows // 8
    span = max(n for n in range(1, min(size, 4) + 1) if size % n == 0)
    vmem = pl.BlockSpec(memory_space=pltpu.VMEM)
    return pl.pallas_call(
        functools.partial(kernel, size, span),
        out_shape=jax.ShapeDtypeStruct((rows, heads, width), BF16),
        in_specs=[vmem] * 3,
        out_specs=vmem,
        scratch_shapes=[
            pltpu.VMEM((2, size, own, heads, width), BF16),
            pltpu.VMEM((2, BLOCK, heads, width), BF16),
            pltpu.VMEM((2, 80, heads, width), BF16),
            pltpu.VMEM((2, 80, heads, width), BF16),
            pltpu.VMEM((heads, rows, width), BF16),
            pltpu.VMEM((2, heads, rows + BLOCK, width), BF16),
            pltpu.VMEM((2, heads, rows // 2, width), BF16),
            pltpu.VMEM((2, heads, rows // 4, width), BF16),
            pltpu.VMEM((2, heads, size * own, width), BF16),
            pltpu.VMEM((rows // HALF, HALF, NEAR), F32),
            pltpu.VMEM((heads, rows, width), F32),
            pltpu.VMEM((heads, rows, width), F32),
            pltpu.VMEM((heads, rows, width), F32),
            pltpu.VMEM((80 * heads, width), F32),
            pltpu.VMEM((HALF * heads, width), F32),
            pltpu.SemaphoreType.DMA((2, 2)),
            pltpu.SemaphoreType.DMA((2, 2)),
            pltpu.SemaphoreType.DMA((2, size)),
            pltpu.SemaphoreType.DMA((2, size)),
            pltpu.SemaphoreType.DMA((2, size)),
            pltpu.SemaphoreType.DMA((2, size)),
        ],
        compiler_params=pltpu.CompilerParams(
            collective_id=0, has_side_effects=True, vmem_limit_bytes=60 * 2**20),
    )(queries, keys, values)


def solution(mesh):
    spec = P(("groups", "seq"), "heads", None)
    return jax.shard_map(
        functools.partial(shards, mesh.shape["seq"]),
        mesh=mesh, in_specs=(spec,) * 3, out_specs=spec, check_vma=False)
```
